256 devices in a mesh: batch: 32 (over z, y_hi, core), seq: 8 (over x, y_lo).
Axes of the slice: x: 4, y: 4 (y_hi: 2, y_lo: 2; y = y_hi * 2 + y_lo), z: 8, core: 2. Of those that a mesh axis runs over, the one named last changes fastest.
Arguments:
- queries: bfloat16 [32768, 4096], P(('batch', 'seq')), parts along dimension 0, may hold values from -130 to 130
- span_keys: bfloat16 [32768, 1024], P(('batch', 'seq')), parts along dimension 0, may hold values from -6 to 6
- span_values: bfloat16 [32768, 1024], P(('batch', 'seq')), parts along dimension 0, may hold values from -6 to 6
- cache_keys: bfloat16 [131072, 1024], P(('batch', 'seq')), parts along dimension 0, may hold values from -6 to 6
- cache_values: bfloat16 [131072, 1024], P(('batch', 'seq')), parts along dimension 0, may hold values from -6 to 6
- span_start: int32 [32], P('batch'), parts along dimension 0, may hold values from 2048 to 16383, as said below
- prompt_length: int32 [32], P('batch'), parts along dimension 0, may hold values from 2304 to 17407, as said below
- window_size: int32 [32], P('batch'), parts along dimension 0, may hold values from 2048 to 4096
Outputs:
- attended: bfloat16 [32768, 4096], P(('batch', 'seq')), parts along dimension 0
The draws below stay inside these ranges and needn't reach their ends.
There are 32 independent parts, one for each index of `batch`. The reference program is written for one: setup_inputs(seed, part) draws one part's arguments, and reference() takes and returns one part's arrays. A program takes and returns all parts, laid end to end along the dimension named above; each array names one. Nothing has to cross between parts.
Inputs may be any that keep to these rules, and one draw needn't show every extreme that they name: Cache row j holds position span_start - 4096 + j and is unused where that is negative. `prompt_length`: lies between span_start + 256 and span_start + 1024; block rows at or past it are padding.
All inputs are finite; a program needn't handle non-finite values.
Results may differ from the reference program's by a relative error of at most 0.0065.
Values may be sent and summed in bfloat16 or wider, within the bound.
No kernel may reach another device: no remote copies, remote signals or barrier semaphores. Data moves between devices by JAX's collectives and lax.ppermute only.
A program may use at most 128 MiB of HBM per device.

```python
import jax
import jax.numpy as jnp
from jax import lax

H = 32
KVH = 8
HD = 128
WINDOW = 4096
SPAN = 1024


def start_and_length(key):
    first, second = jax.random.split(jax.random.fold_in(key, 11))
    begin = jax.random.randint(first, (1,), WINDOW // 2, 4 * WINDOW, dtype=jnp.int32)
    count = jax.random.randint(second, (1,), SPAN // 4, SPAN + 1, dtype=jnp.int32)
    return (begin, begin + count)


def draw_span_start(key, part):
    return start_and_length(key)[0]


def draw_prompt_length(key, part):
    return start_and_length(key)[1]


def draw_window_size(key, part):
    return jax.random.randint(jax.random.fold_in(key, 41), (1,), WINDOW // 2, WINDOW + 1, dtype=jnp.int32)


def draw_span_keys(key, part):
    base = jax.random.truncated_normal(jax.random.fold_in(key, 21), -5.0, 5.0, (SPAN, KVH * HD), jnp.float32)
    return base.astype(jnp.bfloat16)


def draw_queries(key, part):
    return jax.random.truncated_normal(jax.random.fold_in(key, 31), -5.0, 5.0, (SPAN, H * HD), jnp.float32).astype(jnp.bfloat16)


def block_scale(stream_key, dims, pieces, low, high):
    loudness, own = 1.0, jax.random.fold_in(stream_key, 6)
    for position, shards_of in pieces:
        draws = jnp.exp(jax.random.uniform(jax.random.fold_in(own, position), (shards_of,), jnp.float32, low / len(pieces), high / len(pieces)))
        loudness = loudness * jnp.repeat(draws, dims[position] // shards_of).reshape([-1 if axis == position else 1 for axis in range(len(dims))])
    return loudness


def bell_draw(stream_key, dims, spread, reach, cuts=(), kind=jnp.bfloat16):
    factor_of = block_scale(stream_key, dims, cuts, -0.22, 0.18) if cuts else 1.0
    array = jax.random.normal(stream_key, dims, jnp.float32) * spread * factor_of
    return jnp.minimum(jnp.maximum(array, -reach), reach).astype(kind)


def setup_inputs(seed: int = 0, part: int = 0) -> dict:
    seeds = jax.random.split(jax.random.key(seed), 9)
    part_keys = jax.random.split(jax.random.fold_in(seeds[8], part), 9)
    return {
        "queries": draw_queries(jax.random.fold_in(jax.random.fold_in(seeds[8], part), 71), part),
        "span_keys": draw_span_keys(jax.random.fold_in(jax.random.fold_in(seeds[8], part), 71), part),
        "span_values": bell_draw(part_keys[2], (SPAN, KVH * HD), 1.0, 6.0, ((0, 8),)),
        "cache_keys": bell_draw(part_keys[3], (WINDOW, KVH * HD), 1.0, 6.0, ((0, 8),)),
        "cache_values": bell_draw(part_keys[4], (WINDOW, KVH * HD), 1.0, 6.0, ((0, 8),)),
        "span_start": draw_span_start(jax.random.fold_in(jax.random.fold_in(seeds[8], part), 71), part),
        "prompt_length": draw_prompt_length(jax.random.fold_in(jax.random.fold_in(seeds[8], part), 71), part),
        "window_size": draw_window_size(jax.random.fold_in(jax.random.fold_in(seeds[8], part), 71), part),
    }


NEG = -1.0e30


def reference(queries, span_keys, span_values, cache_keys, cache_values, span_start, prompt_length, window_size):
    groups = H // KVH
    scale = HD ** -0.5
    start = span_start[0]
    live = prompt_length[0] - start
    window = window_size[0]
    keys = jnp.concatenate([cache_keys, span_keys], 0).reshape(-1, KVH, HD).astype(jnp.float32)
    values = jnp.concatenate([cache_values, span_values], 0).reshape(-1, KVH, HD).astype(jnp.float32)
    key_pos = jnp.concatenate([start - WINDOW + jnp.arange(WINDOW, dtype=jnp.int32), start + jnp.arange(SPAN, dtype=jnp.int32)]).astype(jnp.int32)
    rows = jnp.arange(SPAN, dtype=jnp.int32)
    query_pos = start + rows
    query_live = rows < live
    diff = query_pos[:, None] - key_pos[None, :]
    valid = (key_pos >= 0)[None, :] & (diff >= 0) & (diff < window) & query_live[:, None]
    grouped = queries.reshape(SPAN, KVH, groups, HD).astype(jnp.float32)

    def one_head(item):
        head_q, head_k, head_v = item
        scores = jnp.einsum('qgd,nd->qgn', head_q, head_k) * scale
        allowed = valid[:, None, :]
        masked = jnp.where(allowed, scores, NEG)
        top = jnp.max(masked, axis=-1, keepdims=True)
        weights = jnp.where(allowed, jnp.exp(scores - top), 0.0)
        total = jnp.sum(weights, axis=-1)
        mixed = jnp.einsum('qgn,nd->qgd', weights.astype(jnp.bfloat16).astype(jnp.float32), head_v)
        safe = jnp.where(query_live[:, None], total, 1.0)
        return jnp.where(query_live[:, None, None], mixed / safe[..., None], 0.0)

    heads = lax.map(one_head, (grouped.transpose(1, 0, 2, 3), keys.transpose(1, 0, 2), values.transpose(1, 0, 2)))
    return heads.transpose(1, 0, 2, 3).reshape(SPAN, H * HD).astype(jnp.bfloat16)
```

```python
import math

import jax
import jax.numpy as jnp
from jax import lax
from jax.experimental import pallas as pl
from jax.experimental.pallas import tpu as pltpu
from jax.sharding import PartitionSpec as P

NEG=-1e30
C=512
def attn_body(start_ref, plen_ref, win_ref, recv, out_ref, q_s, k_s, v_s, S, mx, acc, sems):
    copies=[]
    n=0
    def cp(src,dst):
        nonlocal n
        c=pltpu.make_async_copy(src,dst,sems.at[n]); n+=1
        c.start(); copies.append(c)
    for s in range(8):
        cp(recv.at[s,pl.ds(0,512)],q_s.at[s])
        cp(recv.at[s,pl.ds(512,512)],k_s.at[pl.ds(s*512,512)])
        cp(recv.at[s,pl.ds(1024,512)],v_s.at[pl.ds(s*512,512),pl.ds(0,128)])
        cp(recv.at[s,pl.ds(1536,128)],k_s.at[pl.ds(4096+s*128,128)])
        cp(recv.at[s,pl.ds(1664,128)],v_s.at[pl.ds(4096+s*128,128),pl.ds(0,128)])
    v_s[:,128:256]=jnp.ones((5120,128),jnp.bfloat16)
    start=start_ref[0]; live=plen_ref[0]-start; win=win_ref[0]
    kmin=jnp.maximum(4096-start,0)
    groups=jnp.minimum((live+127)//128,8)
    scale=(128**-0.5)*math.log2(math.e)
    def clo(s): return jnp.maximum(jnp.maximum(4096+s*128-win+1,kmin),0)//C
    def chi(s): return (4096+s*128+127)//C
    for c in copies: c.wait()
    def p1(s,c):
        b=lax.rem(s,2)
        q=q_s[s]; k=k_s[pl.ds(pl.multiple_of(c*C,C),C),:]
        sc=lax.dot_general(q,k,(((1,),(1,)),((),())),preferred_element_type=jnp.float32)
        i=lax.broadcasted_iota(jnp.int32,(128,C),0); kk=lax.broadcasted_iota(jnp.int32,(128,C),1)
        t=i-kk+(4096+s*128-c*C)
        ok=(t>=0)&(t<win)&(kk>=kmin-c*C)
        sc=jnp.where(ok[None],sc.reshape(4,128,C),NEG).reshape(512,C)
        S[b,c]=sc
        m=sc[:,0:128]
        for j in range(1,C//128): m=jnp.maximum(m,sc[:,j*128:(j+1)*128])
        mx[b]=jnp.maximum(mx[b],m)
    def p2(s,c):
        b=lax.rem(s,2)
        m=mx[b]
        p=jnp.exp2((S[b,c]-jnp.tile(m,(1,C//128)))*scale).astype(jnp.bfloat16)
        v=v_s[pl.ds(pl.multiple_of(c*C,C),C),:]
        acc[...]+=jnp.dot(p,v,preferred_element_type=jnp.float32)
    def init(s):
        mx[lax.rem(s,2)]=jnp.full((512,128),NEG,jnp.float32)
    def top(s):
        b=lax.rem(s,2)
        mx[b]=jnp.broadcast_to(jnp.max(mx[b],axis=1,keepdims=True),(512,128))
    def fin(s):
        a=acc[...]
        o=a[:,0:128]/a[:,128:256]
        i=lax.broadcasted_iota(jnp.int32,(4,128,128),1).reshape(512,128)
        out_ref[s]=jnp.where(i+s*128<live,o,0.0).astype(jnp.bfloat16)
    init(0)
    lax.fori_loop(clo(0),chi(0)+1,lambda c,_:(p1(0,c),0)[1],0)
    top(0)
    def stage(t,_):
        s1=t; s2=t-1
        init(s1)
        acc[...]=jnp.zeros_like(acc)
        a,bb=clo(s1),chi(s2)+1
        lax.fori_loop(clo(s2),a,lambda c,_:(p2(s2,c),0)[1],0)
        def both(c,_):
            p1(s1,c); p2(s2,c); return 0
        lax.fori_loop(a,bb,both,0)
        lax.fori_loop(bb,chi(s1)+1,lambda c,_:(p1(s1,c),0)[1],0)
        top(s1)
        fin(s2)
        return 0
    lax.fori_loop(1,groups,stage,0)
    last=groups-1
    acc[...]=jnp.zeros_like(acc)
    lax.fori_loop(clo(last),chi(last)+1,lambda c,_:(p2(last,c),0)[1],0)
    fin(last)
    def dead(s,_):
        out_ref[s]=jnp.zeros((512,128),jnp.bfloat16); return 0
    lax.fori_loop(groups,8,dead,0)

def attn(start,plen,win,recv):
    return pl.pallas_call(attn_body,
        out_shape=jax.ShapeDtypeStruct((8,512,128),jnp.bfloat16),
        in_specs=[pl.BlockSpec(memory_space=pltpu.SMEM)]*3+[pl.BlockSpec(memory_space=pl.ANY)],
        out_specs=pl.BlockSpec(memory_space=pltpu.VMEM),
        scratch_shapes=[pltpu.VMEM((8,512,128),jnp.bfloat16),pltpu.VMEM((5120,128),jnp.bfloat16),pltpu.VMEM((5120,256),jnp.bfloat16),
            pltpu.VMEM((2,10,512,C),jnp.float32),pltpu.VMEM((2,512,128),jnp.float32),pltpu.VMEM((512,256),jnp.float32),pltpu.SemaphoreType.DMA((40,))],
        compiler_params=pltpu.CompilerParams(vmem_limit_bytes=50<<20),
        cost_estimate=pl.CostEstimate(flops=2*2*4096*4352*128,bytes_accessed=5<<20,transcendentals=4096*4352),
        name="attend")(start,plen,win,recv)


def pack_body(q, sk, sv, ck, cv, out, sems):
    copies = []

    def cp(src, dst):
        c = pltpu.make_async_copy(src, dst, sems.at[len(copies)])
        c.start()
        copies.append(c)

    for d in range(8):
        for h in range(4):
            cp(q.at[:, pl.ds((d * 4 + h) * 128, 128)], out.at[d, pl.ds(h * 128, 128)])
        cols = pl.ds(d * 128, 128)
        cp(ck.at[:, cols], out.at[d, pl.ds(512, 512)])
        cp(cv.at[:, cols], out.at[d, pl.ds(1024, 512)])
        cp(sk.at[:, cols], out.at[d, pl.ds(1536, 128)])
        cp(sv.at[:, cols], out.at[d, pl.ds(1664, 128)])
    for c in copies:
        c.wait()


def pack(*arrays):
    return pl.pallas_call(
        pack_body,
        out_shape=jax.ShapeDtypeStruct((8, 1792, 128), jnp.bfloat16),
        in_specs=[pl.BlockSpec(memory_space=pl.ANY)] * 5,
        out_specs=pl.BlockSpec(memory_space=pl.ANY),
        scratch_shapes=[pltpu.SemaphoreType.DMA((64,))],
        name="pack",
    )(*arrays)


def unpack_body(x, out, sems):
    copies = []
    for s in range(8):
        for h in range(4):
            c = pltpu.make_async_copy(
                x.at[s, pl.ds(h * 128, 128)],
                out.at[:, pl.ds((s * 4 + h) * 128, 128)],
                sems.at[len(copies)],
            )
            c.start()
            copies.append(c)
    for c in copies:
        c.wait()


def unpack(x):
    return pl.pallas_call(
        unpack_body,
        out_shape=jax.ShapeDtypeStruct((128, 4096), jnp.bfloat16),
        in_specs=[pl.BlockSpec(memory_space=pl.ANY)],
        out_specs=pl.BlockSpec(memory_space=pl.ANY),
        scratch_shapes=[pltpu.SemaphoreType.DMA((32,))],
        name="unpack",
    )(x)


def body(queries, span_keys, span_values, cache_keys, cache_values, span_start, prompt_length, window_size):
    sent = pack(queries, span_keys, span_values, cache_keys, cache_values)
    got = lax.all_to_all(sent, "seq", split_axis=0, concat_axis=0, tiled=True)
    mixed = attn(span_start, prompt_length, window_size, got)
    back = lax.all_to_all(mixed, "seq", split_axis=0, concat_axis=0, tiled=True)
    return unpack(back)


def solution(mesh):
    rows = P(("batch", "seq"), None)
    placed = (rows,) * 5 + (P("batch"),) * 3
    return jax.shard_map(body, mesh=mesh, in_specs=placed, out_specs=rows, check_vma=False)
```

```python
import math

import jax
import jax.numpy as jnp
from jax import lax
from jax.experimental import pallas as pl
from jax.experimental.pallas import tpu as pltpu
from jax.sharding import PartitionSpec as P

NEG=-1e30
C=512
U=2
KT=0; HS=1
NC=5120//C
SCALE=(128**-0.5)*math.log2(math.e)
def attn_body(start_ref, plen_ref, win_ref, recv, out_ref, k_s, v_s, S0, S1, mx0, mx1, acc, tot):
    S=(S0,S1); mx=(mx0,mx1)
    for s in range(8):
        k_s[s*512:(s+1)*512]=recv[s,512:1024]
        v_s[s*512:(s+1)*512]=recv[s,1024:1536]
        k_s[4096+s*128:4224+s*128]=recv[s,1536:1664]
        v_s[4096+s*128:4224+s*128]=recv[s,1664:1792]
    start=start_ref[0]; live=plen_ref[0]-start; win=win_ref[0]
    kmin=jnp.maximum(4096-start,0)
    groups=jnp.minimum((live+127)//128,8)
    def low(s): return jnp.maximum(jnp.maximum(4096+s*128-win+1,kmin),0)
    def clo(s): return low(s)//C
    def chi(s): return (4096+s*128+127)//C
    def p1(s,b,c,masked):
        k=k_s[pl.ds(pl.multiple_of(c*C,C),C),:]
        R=512//HS
        if masked:
            i=lax.broadcasted_iota(jnp.int32,(128,C),0); kk=lax.broadcasted_iota(jnp.int32,(128,C),1)
            t=i-kk+(4096+s*128-c*C)
            ok=(t>=0)&(t<win)&(kk>=kmin-c*C)
        for h in range(HS):
            q=recv[s,h*R:(h+1)*R]
            sc=lax.dot_general(q,k,(((1,),(1,)),((),())),preferred_element_type=jnp.float32)
            if masked:
                sc=jnp.where(ok[None],sc.reshape(R//128,128,C),NEG).reshape(R,C)
            S[b][c,h*R:(h+1)*R]=sc
            m=sc[:,0:128]
            for j in range(1,C//128): m=jnp.maximum(m,sc[:,j*128:(j+1)*128])
            mx[b][h*R:(h+1)*R]=jnp.maximum(mx[b][h*R:(h+1)*R],m)
    def p2(b,c):
        v=v_s[pl.ds(pl.multiple_of(c*C,C),C),:]
        R=512//HS
        for h in range(HS):
            r=slice(h*R,(h+1)*R)
            m=mx[b][r]
            p=jnp.exp2((S[b][c,r]-jnp.tile(m,(1,C//128)))*SCALE)
            t=p[:,0:128]
            for j in range(1,C//128): t=t+p[:,j*128:(j+1)*128]
            tot[r]+=t
            acc[r]+=jnp.dot(p.astype(jnp.bfloat16),v,preferred_element_type=jnp.float32)
    def init(b): mx[b][...]=jnp.full((512,128),NEG,jnp.float32)
    def zero():
        acc[...]=jnp.zeros_like(acc); tot[...]=jnp.zeros_like(tot)
    def top(b): mx[b][...]=jnp.broadcast_to(jnp.max(mx[b][...],axis=1,keepdims=True),(512,128))
    def fin(s):
        o=acc[...]/jnp.sum(tot[...],axis=1,keepdims=True)
        i=lax.broadcasted_iota(jnp.int32,(4,128,128),1).reshape(512,128)
        out_ref[s]=jnp.where(i+s*128<live,o,0.0).astype(jnp.bfloat16)
    def loop(a,b,f): lax.fori_loop(a,b,lambda c,_:(f(c),0)[1],0)
    def stage(s1,s2,b1,b2):
        init(b1); zero()
        a,e1,e2=clo(s1),chi(s1),chi(s2)
        loop(clo(s2),a,lambda c:p2(b2,c))
        lo=jnp.maximum((low(s1)+127+C-1)//C,a)
        hi=jnp.minimum(e1,e2+1)
        def edge(j):
            c=jnp.where(j<lo,j,j-lo+hi)
            p1(s1,b1,c,True); p2(b2,c)
        loop(a,lo+e2+1-hi,edge)
        def inner(c):
            for u in range(U): p1(s1,b1,c+u,False)
            for u in range(U): p2(b2,c+u)
        n=(hi-lo)//U
        loop(0,n,lambda j:inner(lo+U*j))
        def rest(c):
            p1(s1,b1,c,False); p2(b2,c)
        loop(lo+n*U,hi,rest)
        loop(e2+1,e1+1,lambda c:p1(s1,b1,c,True))
        top(b1); fin(s2)
    init(0)
    loop(clo(0),chi(0)+1,lambda c:p1(0,0,c,True))
    top(0)
    def pair(u,_):
        t=2*u+1
        @pl.when(t<groups)
        def _(): stage(t,t-1,1,0)
        @pl.when(t+1<groups)
        def _(): stage(t+1,t,0,1)
        return 0
    lax.fori_loop(0,groups//2,pair,0)
    last=groups-1
    zero()
    @pl.when(lax.rem(last,2)==0)
    def _(): loop(clo(last),chi(last)+1,lambda c:p2(0,c))
    @pl.when(lax.rem(last,2)==1)
    def _(): loop(clo(last),chi(last)+1,lambda c:p2(1,c))
    fin(last)
    def dead(s): out_ref[s]=jnp.zeros((512,128),jnp.bfloat16)
    loop(groups,8,dead)

def attn(start,plen,win,recv):
    return pl.pallas_call(attn_body,
        out_shape=jax.ShapeDtypeStruct((8,512,128),jnp.bfloat16),
        in_specs=[pl.BlockSpec(memory_space=pltpu.SMEM)]*3+[pl.BlockSpec(memory_space=pltpu.VMEM)],
        out_specs=pl.BlockSpec(memory_space=pltpu.VMEM),
        scratch_shapes=[pltpu.VMEM((5120,128),jnp.bfloat16),pltpu.VMEM((5120,128),jnp.bfloat16),
            pltpu.VMEM((NC,512,C),jnp.float32),pltpu.VMEM((NC,512,C),jnp.float32),pltpu.VMEM((512,128),jnp.float32),pltpu.VMEM((512,128),jnp.float32),
            pltpu.VMEM((512,128),jnp.float32),pltpu.VMEM((512,128),jnp.float32)],
        compiler_params=pltpu.CompilerParams(vmem_limit_bytes=40<<20),
        cost_estimate=pl.CostEstimate(flops=2*2*4096*4352*128,bytes_accessed=5<<20,transcendentals=4096*4352),
        name="attend")(start,plen,win,recv)


def pack_body(q, sk, sv, ck, cv, out, qv, skv, svv, ckv, cvv, in_sems, sems):
    loads = [
        pltpu.make_async_copy(a, b, in_sems.at[i])
        for i, (a, b) in enumerate([(q, qv), (ck, ckv), (cv, cvv), (sk, skv), (sv, svv)])
    ]
    for c in loads:
        c.start()
    stores = []

    def cp(src, dst):
        c = pltpu.make_async_copy(src, dst, sems.at[len(stores)])
        c.start()
        stores.append(c)

    loads[0].wait()
    for e in range(8):
        for h in range(4):
            cp(qv.at[:, pl.ds((e * 4 + h) * 128, 128)], out.at[e, pl.ds(h * 128, 128)])
    for i, (v, at, count) in enumerate([(ckv, 512, 512), (cvv, 1024, 512), (skv, 1536, 128), (svv, 1664, 128)]):
        loads[1 + i].wait()
        for e in range(8):
            cp(v.at[:, pl.ds(e * 128, 128)], out.at[e, pl.ds(at, count)])
    for c in stores:
        c.wait()


def pack(*arrays):
    return pl.pallas_call(
        pack_body,
        out_shape=jax.ShapeDtypeStruct((8, 1792, 128), jnp.bfloat16),
        in_specs=[pl.BlockSpec(memory_space=pl.ANY)] * 5,
        out_specs=pl.BlockSpec(memory_space=pl.ANY),
        scratch_shapes=[pltpu.VMEM(a.shape, a.dtype) for a in arrays]
        + [pltpu.SemaphoreType.DMA((5,)), pltpu.SemaphoreType.DMA((64,))],
        compiler_params=pltpu.CompilerParams(vmem_limit_bytes=16 << 20),
        name="pack",
    )(*arrays)


def unpack_body(x, out):
    for s in range(x.shape[0]):
        for h in range(4):
            at = (s * 4 + h) * 128
            out[:, at : at + 128] = x[s, h * 128 : (h + 1) * 128]


def unpack(x):
    return pl.pallas_call(
        unpack_body,
        grid=(2,),
        out_shape=jax.ShapeDtypeStruct((128, 4096), jnp.bfloat16),
        in_specs=[pl.BlockSpec((4, 512, 128), lambda i: (i, 0, 0))],
        out_specs=pl.BlockSpec((128, 2048), lambda i: (0, i)),
        compiler_params=pltpu.CompilerParams(vmem_limit_bytes=16 << 20),
        name="unpack",
    )(x)


def body(queries, span_keys, span_values, cache_keys, cache_values, span_start, prompt_length, window_size):
    sent = pack(queries, span_keys, span_values, cache_keys, cache_values)
    got = lax.all_to_all(sent, "seq", split_axis=0, concat_axis=0, tiled=True)
    mixed = attn(span_start, prompt_length, window_size, got)
    back = lax.all_to_all(mixed, "seq", split_axis=0, concat_axis=0, tiled=True)
    return unpack(back)


def solution(mesh):
    rows = P(("batch", "seq"), None)
    placed = (rows,) * 5 + (P("batch"),) * 3
    return jax.shard_map(body, mesh=mesh, in_specs=placed, out_specs=rows, check_vma=False)
```

```python
import math

import jax
import jax.numpy as jnp
import numpy as np
from jax import lax
from jax.experimental import pallas as pl
from jax.experimental.pallas import tpu as pltpu
from jax.sharding import PartitionSpec as P

NEG=-1e30
C=512
A=384
B=512-A
U1=2
U2=2
G=512
R1=G+2*A
R2=2*B+256
SCALE=(128**-0.5)*math.log2(math.e)


def positions(first):
    source=np.arange(8)[:,None]*512
    if first:
        p=(source+np.arange(A)[None]).reshape(-1)
    else:
        p=np.concatenate([(source+A+np.arange(B)[None]).reshape(-1),4096+np.arange(1024)])
    return p.reshape(-1,C).astype(np.int32)


def attend_body(first,start_ref,plen_ref,win_ref,pos_ref,got1,*rest):
    if first:
        state,q_s,k_s,v_s,S0,S1,mx0,mx1,acc,tot,acc_v,m_v,t_v,sems,group_sems=rest
        states=((acc_v,state.at[0]),(m_v,state.at[1]),(t_v,state.at[2]))
        U=U1
    else:
        got2,state,out_ref,q_s,k_s,v_s,S0,S1,mx0,mx1,acc,tot,acc_v,m_v,t_v,sems,group_sems=rest
        states=((state.at[0],acc_v),(state.at[1],m_v),(state.at[2],t_v))
        U=U2
    S=(S0,S1)
    mx=(mx0,mx1)
    pos=positions(first)
    mins=[int(x) for x in pos[:,0]]
    maxs=[int(x) for x in pos[:,-1]]
    early=[]
    late=[]

    def cp(src,dst,to):
        c=pltpu.make_async_copy(src,dst,sems.at[len(early)+len(late)])
        c.start()
        to.append(c)

    for s in range(8):
        if first:
            cp(got1.at[s,pl.ds(G,A)],k_s.at[pl.ds(s*A,A)],early)
        else:
            cp(got2.at[s,pl.ds(0,B)],k_s.at[pl.ds(s*B,B)],early)
            cp(got2.at[s,pl.ds(2*B,128)],k_s.at[pl.ds(8*B+s*128,128)],early)
    start=start_ref[0]
    live=plen_ref[0]-start
    win=win_ref[0]
    kmin=jnp.maximum(4096-start,0)
    groups=jnp.minimum((live+127)//128,8)

    def state_copies(s):
        return [pltpu.make_async_copy(a.at[s],b.at[s],group_sems.at[1+i,s]) for i,(a,b) in enumerate(states)]

    def group_copies(s):
        own=pltpu.make_async_copy(got1.at[s,pl.ds(0,G)],q_s.at[s],group_sems.at[0,s])
        return [own] if first else [own]+state_copies(s)

    for s in range(8):
        @pl.when(s<groups)
        def _():
            for c in group_copies(s):
                c.start()

    for s in range(8):
        if first:
            cp(got1.at[s,pl.ds(G+A,A)],v_s.at[pl.ds(s*A,A)],late)
        else:
            cp(got2.at[s,pl.ds(B,B)],v_s.at[pl.ds(s*B,B)],late)
            cp(got2.at[s,pl.ds(2*B+128,128)],v_s.at[pl.ds(8*B+s*128,128)],late)

    def count(tests):
        return sum(jnp.asarray(t).astype(jnp.int32) for t in tests)

    def low(s):
        return jnp.maximum(4096+s*128-win+1,kmin)

    def spans(s):
        l=low(s)
        q0=4096+s*128
        a=count([l>m for m in maxs])
        lo=jnp.maximum(count([l+127>m for m in mins]),a)
        hi=count([q0>=m for m in maxs])
        e=count([q0+127>=m for m in mins])
        return a,lo,hi,e

    def p1(s,b,c,masked):
        k=k_s[pl.ds(pl.multiple_of(c*C,C),C),:]
        sc=lax.dot_general(q_s[s],k,(((1,),(1,)),((),())),preferred_element_type=jnp.float32)
        if masked:
            at=pos_ref[c]
            t=lax.broadcasted_iota(jnp.int32,(128,C),0)+(4096+s*128)-at
            ok=(t>=0)&(t<win)&(at>=kmin)
            sc=jnp.where(ok[None],sc.reshape(4,128,C),NEG).reshape(512,C)
        S[b][c]=sc
        m=sc[:,0:128]
        for j in range(1,C//128):
            m=jnp.maximum(m,sc[:,j*128:(j+1)*128])
        mx[b][...]=jnp.maximum(mx[b][...],m)

    def p2(b,c):
        v=v_s[pl.ds(pl.multiple_of(c*C,C),C),:]
        p=jnp.exp2((S[b][c]-jnp.tile(mx[b][...],(1,C//128)))*SCALE)
        t=p[:,0:128]
        for j in range(1,C//128):
            t=t+p[:,j*128:(j+1)*128]
        tot[...]+=t
        acc[...]+=jnp.dot(p.astype(jnp.bfloat16),v,preferred_element_type=jnp.float32)

    def init(s,b):
        for c in group_copies(s):
            c.wait()
        mx[b][...]=jnp.full((512,128),NEG,jnp.float32) if first else m_v[s]

    def zero():
        acc[...]=jnp.zeros_like(acc)
        tot[...]=jnp.zeros_like(tot)

    def top(b):
        mx[b][...]=jnp.broadcast_to(jnp.max(mx[b][...],axis=1,keepdims=True),(512,128))

    def fin(s,b):
        if first:
            acc_v[s]=acc[...]
            m_v[s]=mx[b][...]
            t_v[s]=tot[...]
            for c in state_copies(s):
                c.start()
        else:
            f=jnp.exp2((m_v[s]-mx[b][...])*SCALE)
            total=jnp.sum(tot[...]+f*t_v[s],axis=1,keepdims=True)
            o=(acc[...]+f*acc_v[s])/total
            i=lax.broadcasted_iota(jnp.int32,(4,128,128),1).reshape(512,128)
            out_ref[s]=jnp.where(i+s*128<live,o,0.0).astype(jnp.bfloat16)

    def loop(a,b,f):
        lax.fori_loop(a,b,lambda c,_:(f(c),0)[1],0)

    def stage(s1,b1):
        s2=s1-1
        b2=1-b1
        init(s1,b1)
        zero()
        a2,_,_,e2=spans(s2)
        a,lo,hi,e1=spans(s1)
        loop(a2,a,lambda c:p2(b2,c))
        hi=jnp.maximum(jnp.minimum(hi,e2),lo)

        def edge(j):
            c=jnp.where(j<lo,j,j-lo+hi)
            p1(s1,b1,c,True)
            p2(b2,c)

        loop(a,lo+e2-hi,edge)

        def inner(c):
            for u in range(U):
                p1(s1,b1,c+u,False)
            for u in range(U):
                p2(b2,c+u)

        n=(hi-lo)//U
        loop(0,n,lambda j:inner(lo+U*j))

        def rest(c):
            p1(s1,b1,c,False)
            p2(b2,c)

        loop(lo+n*U,hi,rest)
        loop(e2,e1,lambda c:p1(s1,b1,c,True))
        top(b1)
        fin(s2,b2)

    for c in early:
        c.wait()
    init(0,0)
    a,lo,hi,e=spans(0)
    loop(a,e,lambda c:p1(0,0,c,True))
    top(0)
    for c in late:
        c.wait()

    def pair(u,_):
        t=2*u+1

        @pl.when(t<groups)
        def _():
            stage(t,1)

        @pl.when(t+1<groups)
        def _():
            stage(t+1,0)

        return 0

    lax.fori_loop(0,groups//2,pair,0)
    last=groups-1
    zero()
    a,_,_,e=spans(last)
    for b in range(2):
        @pl.when(lax.rem(last,2)==b)
        def _():
            loop(a,e,lambda c:p2(b,c))
            fin(last,b)

    if first:
        def finish(s):
            for c in state_copies(s):
                c.wait()

        loop(0,groups,finish)
    else:
        def dead(s):
            out_ref[s]=jnp.zeros((512,128),jnp.bfloat16)

        loop(groups,8,dead)


def attend(first,start,plen,win,*arrays):
    keys=8*A if first else 8*B+1024
    state=jax.ShapeDtypeStruct((3,8,512,128),jnp.float32)
    whole=pl.BlockSpec(memory_space=pltpu.VMEM)
    there=pl.BlockSpec(memory_space=pl.ANY)
    pos=jnp.asarray(positions(first)[:,None])
    return pl.pallas_call(
        lambda *refs: attend_body(first,*refs),
        out_shape=state if first else jax.ShapeDtypeStruct((8,512,128),jnp.bfloat16),
        in_specs=[pl.BlockSpec(memory_space=pltpu.SMEM)]*3+[whole]+([there]*(1 if first else 3)),
        out_specs=there if first else whole,
        scratch_shapes=[
            pltpu.VMEM((8,512,128),jnp.bfloat16),
            pltpu.VMEM((keys,128),jnp.bfloat16),
            pltpu.VMEM((keys,128),jnp.bfloat16),
            pltpu.VMEM((keys//C,512,C),jnp.float32),
            pltpu.VMEM((keys//C,512,C),jnp.float32),
            pltpu.VMEM((512,128),jnp.float32),
            pltpu.VMEM((512,128),jnp.float32),
            pltpu.VMEM((512,128),jnp.float32),
            pltpu.VMEM((512,128),jnp.float32),
            pltpu.VMEM((8,512,128),jnp.float32),
            pltpu.VMEM((8,512,128),jnp.float32),
            pltpu.VMEM((8,512,128),jnp.float32),
            pltpu.SemaphoreType.DMA((16 if first else 32,)),
            pltpu.SemaphoreType.DMA((4,8)),
        ],
        compiler_params=pltpu.CompilerParams(vmem_limit_bytes=56<<20),
        cost_estimate=pl.CostEstimate(flops=4*4096*keys*128,bytes_accessed=5<<20,transcendentals=4096*keys),
        name="attend_first" if first else "attend_rest",
    )(start,plen,win,pos,*arrays)


def pack_body(moves, *refs):
    n = max(m[0] for m in moves) + 1
    arrays, out, local, in_sems, sems = refs[:n], refs[n], refs[n + 1 : 2 * n + 1], refs[-2], refs[-1]
    loads = [pltpu.make_async_copy(a, b, in_sems.at[i]) for i, (a, b) in enumerate(zip(arrays, local))]
    for c in loads:
        c.start()
    stores = []
    for i in range(n):
        loads[i].wait()
        for j, first, count, heads, at in moves:
            if i != j:
                continue
            for e in range(8):
                for h in range(heads):
                    c = pltpu.make_async_copy(
                        local[i].at[pl.ds(first, count), pl.ds((e * heads + h) * 128, 128)],
                        out.at[e, pl.ds(at + h * count, count)],
                        sems.at[len(stores)],
                    )
                    c.start()
                    stores.append(c)
    for c in stores:
        c.wait()


def pack(moves, rows, *arrays):
    return pl.pallas_call(
        lambda *refs: pack_body(moves, *refs),
        out_shape=jax.ShapeDtypeStruct((8, rows, 128), jnp.bfloat16),
        in_specs=[pl.BlockSpec(memory_space=pl.ANY)] * len(arrays),
        out_specs=pl.BlockSpec(memory_space=pl.ANY),
        scratch_shapes=[pltpu.VMEM(a.shape, a.dtype) for a in arrays]
        + [pltpu.SemaphoreType.DMA((len(arrays),)), pltpu.SemaphoreType.DMA((8 * sum(m[3] for m in moves),))],
        compiler_params=pltpu.CompilerParams(vmem_limit_bytes=60 << 20),
        cost_estimate=pl.CostEstimate(flops=0, bytes_accessed=4 * 8 * rows * 128 * 2, transcendentals=0),
        name="pack",
    )(*arrays)


def unpack_body(x, out):
    for s in range(x.shape[0]):
        for h in range(4):
            at = (s * 4 + h) * 128
            out[:, at : at + 128] = x[s, h * 128 : (h + 1) * 128]


def unpack(x):
    return pl.pallas_call(
        unpack_body,
        grid=(2,),
        out_shape=jax.ShapeDtypeStruct((128, 4096), jnp.bfloat16),
        in_specs=[pl.BlockSpec((4, 512, 128), lambda i: (i, 0, 0))],
        out_specs=pl.BlockSpec((128, 2048), lambda i: (0, i)),
        compiler_params=pltpu.CompilerParams(vmem_limit_bytes=16 << 20),
        name="unpack",
    )(x)


def body(queries, span_keys, span_values, cache_keys, cache_values, span_start, prompt_length, window_size):
    def swap(x):
        return lax.all_to_all(x, "seq", split_axis=0, concat_axis=0, tiled=True)

    sent1 = pack([(0, 0, 128, 4, 0), (1, 0, A, 1, G), (2, 0, A, 1, G + A)], R1, queries, cache_keys, cache_values)
    sent2 = pack(
        [(0, A, B, 1, 0), (1, A, B, 1, B), (2, 0, 128, 1, 2 * B), (3, 0, 128, 1, 2 * B + 128)],
        R2,
        cache_keys,
        cache_values,
        span_keys,
        span_values,
    )
    scalars = (span_start, prompt_length, window_size)
    got1 = swap(sent1)
    got2 = swap(sent2)
    state = attend(True, *scalars, got1)
    mixed = attend(False, *scalars, got1, got2, state)
    return unpack(swap(mixed))


def solution(mesh):
    rows = P(("batch", "seq"), None)
    placed = (rows,) * 5 + (P("batch"),) * 3
    return jax.shard_map(body, mesh=mesh, in_specs=placed, out_specs=rows, check_vma=False)
```

```python
import math

import jax
import jax.numpy as jnp
from jax import lax
from jax.experimental import pallas as pl
from jax.experimental.pallas import tpu as pltpu
from jax.sharding import PartitionSpec as P

NEG=-1e30
C=512
U=2
QT=0
SCALE=(128**-0.5)*math.log2(math.e)
def attn_body(start_ref, plen_ref, win_ref, recv, out_ref, k_s, v_s, q_s, S0, S1, mx0, mx1, acc, tot, sems):
    S=(S0,S1); mx=(mx0,mx1)
    start=start_ref[0]; live=plen_ref[0]-start; win=win_ref[0]
    kmin=jnp.maximum(4096-start,0)
    groups=jnp.minimum((live+127)//128,8)
    def low(s): return jnp.maximum(4096+s*128-win+1,kmin)
    def clo(s): return low(s)//C
    def chi(s): return (4096+s*128+127)//C
    for s in range(8):
        k_s[s*512:(s+1)*512]=recv[s,512:1024]
        k_s[4096+s*128:4224+s*128]=recv[s,1536:1664]
        v_s[s]=recv[s,1024:1536].T
        v_s[8+s//4,:,(s%4)*128:(s%4+1)*128]=recv[s,1664:1792].T
        if QT: q_s[s]=recv[s,0:512].T
    def p1(s,b,c,masked):
        k=k_s[pl.ds(pl.multiple_of(c*C,C),C),:]
        if QT: sc=jnp.dot(k,q_s[s],preferred_element_type=jnp.float32)
        else: sc=lax.dot_general(k,recv[s,0:512],(((1,),(1,)),((),())),preferred_element_type=jnp.float32)
        if masked:
            row=lax.broadcasted_iota(jnp.int32,(C,128),0); lane=lax.broadcasted_iota(jnp.int32,(C,128),1)
            t=lane-row+(4096+s*128-c*C)
            ok=(t>=0)&(t<win)&(row>=kmin-c*C)
            sc=jnp.concatenate([jnp.where(ok,sc[:,h*128:(h+1)*128],NEG) for h in range(4)],1)
        S[b][c]=sc
        mx[b][...]=jnp.maximum(mx[b][...],jnp.max(sc.reshape(C//8,8,512),axis=0))
    def p2(b,c):
        p=jnp.exp2((S[b][c].reshape(C//8,8,512)-mx[b][...][None])*SCALE)
        tot[...]+=jnp.sum(p,axis=0)
        acc[...]+=jnp.dot(v_s[c],p.reshape(C,512).astype(jnp.bfloat16),preferred_element_type=jnp.float32)
    def init(b): mx[b][...]=jnp.full((8,512),NEG,jnp.float32)
    def zero():
        acc[...]=jnp.zeros_like(acc); tot[...]=jnp.zeros_like(tot)
    def top(b): mx[b][...]=jnp.broadcast_to(jnp.max(mx[b][...],axis=0,keepdims=True),(8,512))
    def fin(s):
        o=acc[...]/jnp.sum(tot[...],axis=0,keepdims=True)
        o=o.T
        i=lax.broadcasted_iota(jnp.int32,(4,128,128),1).reshape(512,128)
        out_ref[s]=jnp.where(i+s*128<live,o,0.0).astype(jnp.bfloat16)
    def loop(a,b,f): lax.fori_loop(a,b,lambda c,_:(f(c),0)[1],0)
    def stage(s1,s2,b1,b2):
        init(b1); zero()
        a,e1,e2=clo(s1),chi(s1),chi(s2)
        loop(clo(s2),a,lambda c:p2(b2,c))
        lo=jnp.maximum((low(s1)+127+C-1)//C,a)
        hi=jnp.minimum(e1,e2+1)
        def edge(j):
            c=jnp.where(j<lo,j,j-lo+hi)
            p1(s1,b1,c,True); p2(b2,c)
        loop(a,lo+e2+1-hi,edge)
        def inner(c):
            for u in range(U): p1(s1,b1,c+u,False)
            for u in range(U): p2(b2,c+u)
        n=(hi-lo)//U
        loop(0,n,lambda j:inner(lo+U*j))
        def rest(c):
            p1(s1,b1,c,False); p2(b2,c)
        loop(lo+n*U,hi,rest)
        loop(e2+1,e1+1,lambda c:p1(s1,b1,c,True))
        top(b1); fin(s2)
    init(0)
    loop(clo(0),chi(0)+1,lambda c:p1(0,0,c,True))
    top(0)
    def pair(u,_):
        t=2*u+1
        @pl.when(t<groups)
        def _(): stage(t,t-1,1,0)
        @pl.when(t+1<groups)
        def _(): stage(t+1,t,0,1)
        return 0
    lax.fori_loop(0,groups//2,pair,0)
    last=groups-1
    zero()
    @pl.when(lax.rem(last,2)==0)
    def _(): loop(clo(last),chi(last)+1,lambda c:p2(0,c))
    @pl.when(lax.rem(last,2)==1)
    def _(): loop(clo(last),chi(last)+1,lambda c:p2(1,c))
    fin(last)
    def dead(s): out_ref[s]=jnp.zeros((512,128),jnp.bfloat16)
    loop(groups,8,dead)

def attn(start,plen,win,recv):
    return pl.pallas_call(attn_body,
        out_shape=jax.ShapeDtypeStruct((8,512,128),jnp.bfloat16),
        in_specs=[pl.BlockSpec(memory_space=pltpu.SMEM)]*3+[pl.BlockSpec(memory_space=pltpu.VMEM)],
        out_specs=pl.BlockSpec(memory_space=pltpu.VMEM),
        scratch_shapes=[pltpu.VMEM((5120,128),jnp.bfloat16),pltpu.VMEM((10,128,512),jnp.bfloat16),pltpu.VMEM((8,128,512),jnp.bfloat16),
            pltpu.VMEM((10,512,C),jnp.float32),pltpu.VMEM((10,512,C),jnp.float32),pltpu.VMEM((8,512),jnp.float32),pltpu.VMEM((8,512),jnp.float32),
            pltpu.VMEM((128,512),jnp.float32),pltpu.VMEM((8,512),jnp.float32),pltpu.SemaphoreType.DMA((40,))],
        compiler_params=pltpu.CompilerParams(vmem_limit_bytes=40<<20),
        cost_estimate=pl.CostEstimate(flops=2*2*4096*4352*128,bytes_accessed=5<<20,transcendentals=4096*4352),
        name="attend")(start,plen,win,recv)


def pack_body(q, sk, sv, ck, cv, out, qv, skv, svv, ckv, cvv, in_sems, sems):
    loads = [
        pltpu.make_async_copy(a, b, in_sems.at[i])
        for i, (a, b) in enumerate([(q, qv), (ck, ckv), (cv, cvv), (sk, skv), (sv, svv)])
    ]
    for c in loads:
        c.start()
    stores = []

    def cp(src, dst):
        c = pltpu.make_async_copy(src, dst, sems.at[len(stores)])
        c.start()
        stores.append(c)

    loads[0].wait()
    for e in range(8):
        for h in range(4):
            cp(qv.at[:, pl.ds((e * 4 + h) * 128, 128)], out.at[e, pl.ds(h * 128, 128)])
    for i, (v, at, count) in enumerate([(ckv, 512, 512), (cvv, 1024, 512), (skv, 1536, 128), (svv, 1664, 128)]):
        loads[1 + i].wait()
        for e in range(8):
            cp(v.at[:, pl.ds(e * 128, 128)], out.at[e, pl.ds(at, count)])
    for c in stores:
        c.wait()


def pack(*arrays):
    return pl.pallas_call(
        pack_body,
        out_shape=jax.ShapeDtypeStruct((8, 1792, 128), jnp.bfloat16),
        in_specs=[pl.BlockSpec(memory_space=pl.ANY)] * 5,
        out_specs=pl.BlockSpec(memory_space=pl.ANY),
        scratch_shapes=[pltpu.VMEM(a.shape, a.dtype) for a in arrays]
        + [pltpu.SemaphoreType.DMA((5,)), pltpu.SemaphoreType.DMA((64,))],
        compiler_params=pltpu.CompilerParams(vmem_limit_bytes=60 << 20),
        name="pack",
    )(*arrays)


def unpack_body(x, out):
    for s in range(x.shape[0]):
        for h in range(4):
            at = (s * 4 + h) * 128
            out[:, at : at + 128] = x[s, h * 128 : (h + 1) * 128]


def unpack(x):
    return pl.pallas_call(
        unpack_body,
        grid=(2,),
        out_shape=jax.ShapeDtypeStruct((128, 4096), jnp.bfloat16),
        in_specs=[pl.BlockSpec((4, 512, 128), lambda i: (i, 0, 0))],
        out_specs=pl.BlockSpec((128, 2048), lambda i: (0, i)),
        compiler_params=pltpu.CompilerParams(vmem_limit_bytes=16 << 20),
        name="unpack",
    )(x)


def body(queries, span_keys, span_values, cache_keys, cache_values, span_start, prompt_length, window_size):
    sent = pack(queries, span_keys, span_values, cache_keys, cache_values)
    got = lax.all_to_all(sent, "seq", split_axis=0, concat_axis=0, tiled=True)
    mixed = attn(span_start, prompt_length, window_size, got)
    back = lax.all_to_all(mixed, "seq", split_axis=0, concat_axis=0, tiled=True)
    return unpack(back)


def solution(mesh):
    rows = P(("batch", "seq"), None)
    placed = (rows,) * 5 + (P("batch"),) * 3
    return jax.shard_map(body, mesh=mesh, in_specs=placed, out_specs=rows, check_vma=False)
```

```python
import math

import jax
import jax.numpy as jnp
from jax import lax
from jax.experimental import pallas as pl
from jax.experimental.pallas import tpu as pltpu
from jax.sharding import PartitionSpec as P

NEG=-1e30
C=512
U=4
V=3
QT=0
SCALE=(128**-0.5)*math.log2(math.e)
def attn_body(start_ref, plen_ref, win_ref, recv, out_ref, k_s, v_s, q_s, S0, S1, mx0, mx1, acc, tot, sems):
    S=(S0,S1); mx=(mx0,mx1)
    start=start_ref[0]; live=plen_ref[0]-start; win=win_ref[0]
    kmin=jnp.maximum(4096-start,0)
    groups=jnp.minimum((live+127)//128,8)
    def low(s): return jnp.maximum(4096+s*128-win+1,kmin)
    def clo(s): return low(s)//C
    def chi(s): return (4096+s*128+127)//C
    for s in range(8):
        k_s[s*512:(s+1)*512]=recv[s,512:1024]
        k_s[4096+s*128:4224+s*128]=recv[s,1536:1664]
        v_s[s]=recv[s,1024:1536].T
        v_s[8+s//4,:,(s%4)*128:(s%4+1)*128]=recv[s,1664:1792].T
        if QT: q_s[s]=recv[s,0:512].T
    def p1(s,b,c,masked):
        k=k_s[pl.ds(pl.multiple_of(c*C,C),C),:]
        if QT: sc=jnp.dot(k,q_s[s],preferred_element_type=jnp.float32)
        else: sc=lax.dot_general(k,recv[s,0:512],(((1,),(1,)),((),())),preferred_element_type=jnp.float32)
        if masked:
            row=lax.broadcasted_iota(jnp.int32,(C,128),0); lane=lax.broadcasted_iota(jnp.int32,(C,128),1)
            t=lane-row+(4096+s*128-c*C)
            ok=(t>=0)&(t<win)&(row>=kmin-c*C)
            sc=jnp.concatenate([jnp.where(ok,sc[:,h*128:(h+1)*128],NEG) for h in range(4)],1)
        S[b][c]=sc
        mx[b][...]=jnp.maximum(mx[b][...],jnp.max(sc.reshape(C//8,8,512),axis=0))
    def p2(b,c):
        p=jnp.exp2((S[b][c].reshape(C//8,8,512)-mx[b][...][None])*SCALE)
        tot[...]+=jnp.sum(p,axis=0)
        acc[...]+=jnp.dot(v_s[c],p.reshape(C,512).astype(jnp.bfloat16),preferred_element_type=jnp.float32)
    def init(b): mx[b][...]=jnp.full((8,512),NEG,jnp.float32)
    def zero():
        acc[...]=jnp.zeros_like(acc); tot[...]=jnp.zeros_like(tot)
    def top(b): mx[b][...]=jnp.broadcast_to(jnp.max(mx[b][...],axis=0,keepdims=True),(8,512))
    def fin(s):
        o=acc[...]/jnp.sum(tot[...],axis=0,keepdims=True)
        o=o.T
        i=lax.broadcasted_iota(jnp.int32,(4,128,128),1).reshape(512,128)
        out_ref[s]=jnp.where(i+s*128<live,o,0.0).astype(jnp.bfloat16)
    def loop(a,b,f): lax.fori_loop(a,b,lambda c,_:(f(c),0)[1],0)
    def unrolled(a,e,f,n=U):
        k=(e-a)//n
        loop(0,k,lambda j:f(a+n*j,n))
        if n>1: loop(a+n*k,e,lambda c:f(c,1))
    def first(c,n):
        for u in range(n): p1(0,0,c+u,True)
    def final(b):
        def f(c,n):
            for u in range(n): p2(b,c+u)
        return f
    def stage(s1,s2,b1,b2):
        init(b1); zero()
        a,e1,e2=clo(s1),chi(s1),chi(s2)
        loop(clo(s2),a,lambda c:p2(b2,c))
        lo=jnp.maximum((low(s1)+127+C-1)//C,a)
        hi=jnp.minimum(e1,e2+1)
        def edge(j):
            c=jnp.where(j<lo,j,j-lo+hi)
            p1(s1,b1,c,True); p2(b2,c)
        loop(a,lo+e2+1-hi,edge)
        def both(c,n):
            for u in range(n):
                p1(s1,b1,c+u,False); p2(b2,c+u)
        n=(hi-lo)//U
        loop(0,n,lambda j:both(lo+U*j,U))
        unrolled(lo+n*U,hi,both,U//2)
        loop(e2+1,e1+1,lambda c:p1(s1,b1,c,True))
        top(b1); fin(s2)
    init(0)
    unrolled(clo(0),chi(0)+1,first,V)
    top(0)
    def pair(u,_):
        t=2*u+1
        @pl.when(t<groups)
        def _(): stage(t,t-1,1,0)
        @pl.when(t+1<groups)
        def _(): stage(t+1,t,0,1)
        return 0
    lax.fori_loop(0,groups//2,pair,0)
    last=groups-1
    zero()
    @pl.when(lax.rem(last,2)==0)
    def _(): unrolled(clo(last),chi(last)+1,final(0),V)
    @pl.when(lax.rem(last,2)==1)
    def _(): unrolled(clo(last),chi(last)+1,final(1),V)
    fin(last)
    def dead(s): out_ref[s]=jnp.zeros((512,128),jnp.bfloat16)
    loop(groups,8,dead)

def attn(start,plen,win,recv):
    return pl.pallas_call(attn_body,
        out_shape=jax.ShapeDtypeStruct((8,512,128),jnp.bfloat16),
        in_specs=[pl.BlockSpec(memory_space=pltpu.SMEM)]*3+[pl.BlockSpec(memory_space=pltpu.VMEM)],
        out_specs=pl.BlockSpec(memory_space=pltpu.VMEM),
        scratch_shapes=[pltpu.VMEM((5120,128),jnp.bfloat16),pltpu.VMEM((10,128,512),jnp.bfloat16),pltpu.VMEM((8,128,512),jnp.bfloat16),
            pltpu.VMEM((10,512,C),jnp.float32),pltpu.VMEM((10,512,C),jnp.float32),pltpu.VMEM((8,512),jnp.float32),pltpu.VMEM((8,512),jnp.float32),
            pltpu.VMEM((128,512),jnp.float32),pltpu.VMEM((8,512),jnp.float32),pltpu.SemaphoreType.DMA((40,))],
        compiler_params=pltpu.CompilerParams(vmem_limit_bytes=40<<20),
        cost_estimate=pl.CostEstimate(flops=2*2*4096*4352*128,bytes_accessed=5<<20,transcendentals=4096*4352),
        name="attend")(start,plen,win,recv)


def pack_body(q, sk, sv, ck, cv, out, qv, skv, svv, ckv, cvv, in_sems, sems):
    loads = [
        pltpu.make_async_copy(a, b, in_sems.at[i])
        for i, (a, b) in enumerate([(q, qv), (ck, ckv), (cv, cvv), (sk, skv), (sv, svv)])
    ]
    for c in loads:
        c.start()
    stores = []

    def cp(src, dst):
        c = pltpu.make_async_copy(src, dst, sems.at[len(stores)])
        c.start()
        stores.append(c)

    loads[0].wait()
    for e in range(8):
        for h in range(4):
            cp(qv.at[:, pl.ds((e * 4 + h) * 128, 128)], out.at[e, pl.ds(h * 128, 128)])
    for i, (v, at, count) in enumerate([(ckv, 512, 512), (cvv, 1024, 512), (skv, 1536, 128), (svv, 1664, 128)]):
        loads[1 + i].wait()
        for e in range(8):
            cp(v.at[:, pl.ds(e * 128, 128)], out.at[e, pl.ds(at, count)])
    for c in stores:
        c.wait()


def pack(*arrays):
    return pl.pallas_call(
        pack_body,
        out_shape=jax.ShapeDtypeStruct((8, 1792, 128), jnp.bfloat16),
        in_specs=[pl.BlockSpec(memory_space=pl.ANY)] * 5,
        out_specs=pl.BlockSpec(memory_space=pl.ANY),
        scratch_shapes=[pltpu.VMEM(a.shape, a.dtype) for a in arrays]
        + [pltpu.SemaphoreType.DMA((5,)), pltpu.SemaphoreType.DMA((64,))],
        compiler_params=pltpu.CompilerParams(vmem_limit_bytes=60 << 20),
        name="pack",
    )(*arrays)


def unpack_body(x, out):
    for s in range(x.shape[0]):
        for h in range(4):
            at = (s * 4 + h) * 128
            out[:, at : at + 128] = x[s, h * 128 : (h + 1) * 128]


def unpack(x):
    return pl.pallas_call(
        unpack_body,
        grid=(2,),
        out_shape=jax.ShapeDtypeStruct((128, 4096), jnp.bfloat16),
        in_specs=[pl.BlockSpec((4, 512, 128), lambda i: (i, 0, 0))],
        out_specs=pl.BlockSpec((128, 2048), lambda i: (0, i)),
        compiler_params=pltpu.CompilerParams(vmem_limit_bytes=16 << 20),
        name="unpack",
    )(x)


def body(queries, span_keys, span_values, cache_keys, cache_values, span_start, prompt_length, window_size):
    sent = pack(queries, span_keys, span_values, cache_keys, cache_values)
    got = lax.all_to_all(sent, "seq", split_axis=0, concat_axis=0, tiled=True)
    mixed = attn(span_start, prompt_length, window_size, got)
    back = lax.all_to_all(mixed, "seq", split_axis=0, concat_axis=0, tiled=True)
    return unpack(back)


def solution(mesh):
    rows = P(("batch", "seq"), None)
    placed = (rows,) * 5 + (P("batch"),) * 3
    return jax.shard_map(body, mesh=mesh, in_specs=placed, out_specs=rows, check_vma=False)
```

```python
import math

import jax
import jax.numpy as jnp
from jax import lax
from jax.experimental import pallas as pl
from jax.experimental.pallas import tpu as pltpu
from jax.sharding import PartitionSpec as P

NEG=-1e30
C=512
U=4
R=3
LIM=40
V=3
QT=0
SCALE=(128**-0.5)*math.log2(math.e)
def attn_body(start_ref, plen_ref, win_ref, recv, out_ref, k_s, v_s, q_s, S0, S1, mx0, mx1, acc, tot, sems):
    S=(S0,S1); mx=(mx0,mx1)
    start=start_ref[0]; live=plen_ref[0]-start; win=win_ref[0]
    kmin=jnp.maximum(4096-start,0)
    groups=jnp.minimum((live+127)//128,8)
    def low(s): return jnp.maximum(4096+s*128-win+1,kmin)
    def clo(s): return low(s)//C
    def chi(s): return (4096+s*128+127)//C
    for s in range(8):
        k_s[s*512:(s+1)*512]=recv[s,512:1024]
        k_s[4096+s*128:4224+s*128]=recv[s,1536:1664]
        v_s[s]=recv[s,1024:1536].T
        v_s[8+s//4,:,(s%4)*128:(s%4+1)*128]=recv[s,1664:1792].T
        if QT: q_s[s]=recv[s,0:512].T
    def p1(s,b,c,masked):
        k=k_s[pl.ds(pl.multiple_of(c*C,C),C),:]
        if QT: sc=jnp.dot(k,q_s[s],preferred_element_type=jnp.float32)
        else: sc=lax.dot_general(k,recv[s,0:512],(((1,),(1,)),((),())),preferred_element_type=jnp.float32)
        if masked:
            row=lax.broadcasted_iota(jnp.int32,(C,128),0); lane=lax.broadcasted_iota(jnp.int32,(C,128),1)
            t=lane-row+(4096+s*128-c*C)
            ok=(t>=0)&(t<win)&(row>=kmin-c*C)
            sc=jnp.concatenate([jnp.where(ok,sc[:,h*128:(h+1)*128],NEG) for h in range(4)],1)
        S[b][c]=sc
        mx[b][...]=jnp.maximum(mx[b][...],jnp.max(sc.reshape(C//8,8,512),axis=0))
    def p2(b,c):
        p=jnp.exp2((S[b][c].reshape(C//8,8,512)-mx[b][...][None])*SCALE)
        tot[...]+=jnp.sum(p,axis=0)
        acc[...]+=jnp.dot(v_s[c],p.reshape(C,512).astype(jnp.bfloat16),preferred_element_type=jnp.float32)
    def init(b): mx[b][...]=jnp.full((8,512),NEG,jnp.float32)
    def zero():
        acc[...]=jnp.zeros_like(acc); tot[...]=jnp.zeros_like(tot)
    def top(b): mx[b][...]=jnp.broadcast_to(jnp.max(mx[b][...],axis=0,keepdims=True),(8,512))
    def fin(s):
        o=acc[...]/jnp.sum(tot[...],axis=0,keepdims=True)
        o=o.T
        i=lax.broadcasted_iota(jnp.int32,(4,128,128),1).reshape(512,128)
        out_ref[s]=jnp.where(i+s*128<live,o,0.0).astype(jnp.bfloat16)
    def loop(a,b,f): lax.fori_loop(a,b,lambda c,_:(f(c),0)[1],0)
    def unrolled(a,e,f,n=U):
        k=(e-a)//n
        loop(0,k,lambda j:f(a+n*j,n))
        if n>1: loop(a+n*k,e,lambda c:f(c,1))
    def first(c,n):
        for u in range(n): p1(0,0,c+u,True)
    def final(b):
        def f(c,n):
            for u in range(n): p2(b,c+u)
        return f
    def stage(s1,s2,b1,b2):
        init(b1); zero()
        a,e1,e2=clo(s1),chi(s1),chi(s2)
        loop(clo(s2),a,lambda c:p2(b2,c))
        lo=jnp.maximum((low(s1)+127+C-1)//C,a)
        hi=jnp.minimum(e1,e2+1)
        def edge(j,n):
            for u in range(n):
                c=jnp.where(j+u<lo,j+u,j+u-lo+hi)
                p1(s1,b1,c,True); p2(b2,c)
        unrolled(a,lo+e2+1-hi,edge,2)
        def both(c,n):
            for u in range(n):
                p1(s1,b1,c+u,False); p2(b2,c+u)
        n=(hi-lo)//U
        loop(0,n,lambda j:both(lo+U*j,U))
        unrolled(lo+n*U,hi,both,R)
        loop(e2+1,e1+1,lambda c:p1(s1,b1,c,True))
        top(b1); fin(s2)
    init(0)
    unrolled(clo(0),chi(0)+1,first,V)
    top(0)
    def pair(u,_):
        t=2*u+1
        @pl.when(t<groups)
        def _(): stage(t,t-1,1,0)
        @pl.when(t+1<groups)
        def _(): stage(t+1,t,0,1)
        return 0
    lax.fori_loop(0,groups//2,pair,0)
    last=groups-1
    zero()
    @pl.when(lax.rem(last,2)==0)
    def _(): unrolled(clo(last),chi(last)+1,final(0),V)
    @pl.when(lax.rem(last,2)==1)
    def _(): unrolled(clo(last),chi(last)+1,final(1),V)
    fin(last)
    def dead(s): out_ref[s]=jnp.zeros((512,128),jnp.bfloat16)
    loop(groups,8,dead)

def attn(start,plen,win,recv):
    return pl.pallas_call(attn_body,
        out_shape=jax.ShapeDtypeStruct((8,512,128),jnp.bfloat16),
        in_specs=[pl.BlockSpec(memory_space=pltpu.SMEM)]*3+[pl.BlockSpec(memory_space=pltpu.VMEM)],
        out_specs=pl.BlockSpec(memory_space=pltpu.VMEM),
        scratch_shapes=[pltpu.VMEM((5120,128),jnp.bfloat16),pltpu.VMEM((10,128,512),jnp.bfloat16),pltpu.VMEM((8,128,512),jnp.bfloat16),
            pltpu.VMEM((10,512,C),jnp.float32),pltpu.VMEM((10,512,C),jnp.float32),pltpu.VMEM((8,512),jnp.float32),pltpu.VMEM((8,512),jnp.float32),
            pltpu.VMEM((128,512),jnp.float32),pltpu.VMEM((8,512),jnp.float32),pltpu.SemaphoreType.DMA((40,))],
        compiler_params=pltpu.CompilerParams(vmem_limit_bytes=LIM<<20),
        cost_estimate=pl.CostEstimate(flops=2*2*4096*4352*128,bytes_accessed=5<<20,transcendentals=4096*4352),
        name="attend")(start,plen,win,recv)


def pack_body(q, sk, sv, ck, cv, out, qv, skv, svv, ckv, cvv, in_sems, sems):
    loads = [
        pltpu.make_async_copy(a, b, in_sems.at[i])
        for i, (a, b) in enumerate([(q, qv), (ck, ckv), (cv, cvv), (sk, skv), (sv, svv)])
    ]
    for c in loads:
        c.start()
    stores = []

    def cp(src, dst):
        c = pltpu.make_async_copy(src, dst, sems.at[len(stores)])
        c.start()
        stores.append(c)

    loads[0].wait()
    for e in range(8):
        for h in range(4):
            cp(qv.at[:, pl.ds((e * 4 + h) * 128, 128)], out.at[e, pl.ds(h * 128, 128)])
    for i, (v, at, count) in enumerate([(ckv, 512, 512), (cvv, 1024, 512), (skv, 1536, 128), (svv, 1664, 128)]):
        loads[1 + i].wait()
        for e in range(8):
            cp(v.at[:, pl.ds(e * 128, 128)], out.at[e, pl.ds(at, count)])
    for c in stores:
        c.wait()


def pack(*arrays):
    return pl.pallas_call(
        pack_body,
        out_shape=jax.ShapeDtypeStruct((8, 1792, 128), jnp.bfloat16),
        in_specs=[pl.BlockSpec(memory_space=pl.ANY)] * 5,
        out_specs=pl.BlockSpec(memory_space=pl.ANY),
        scratch_shapes=[pltpu.VMEM(a.shape, a.dtype) for a in arrays]
        + [pltpu.SemaphoreType.DMA((5,)), pltpu.SemaphoreType.DMA((64,))],
        compiler_params=pltpu.CompilerParams(vmem_limit_bytes=60 << 20),
        name="pack",
    )(*arrays)


def unpack_body(x, out):
    for s in range(x.shape[0]):
        for h in range(4):
            at = (s * 4 + h) * 128
            out[:, at : at + 128] = x[s, h * 128 : (h + 1) * 128]


def unpack(x):
    return pl.pallas_call(
        unpack_body,
        grid=(2,),
        out_shape=jax.ShapeDtypeStruct((128, 4096), jnp.bfloat16),
        in_specs=[pl.BlockSpec((4, 512, 128), lambda i: (i, 0, 0))],
        out_specs=pl.BlockSpec((128, 2048), lambda i: (0, i)),
        compiler_params=pltpu.CompilerParams(vmem_limit_bytes=16 << 20),
        name="unpack",
    )(x)


def body(queries, span_keys, span_values, cache_keys, cache_values, span_start, prompt_length, window_size):
    sent = pack(queries, span_keys, span_values, cache_keys, cache_values)
    got = lax.all_to_all(sent, "seq", split_axis=0, concat_axis=0, tiled=True)
    mixed = attn(span_start, prompt_length, window_size, got)
    back = lax.all_to_all(mixed, "seq", split_axis=0, concat_axis=0, tiled=True)
    return unpack(back)


def solution(mesh):
    rows = P(("batch", "seq"), None)
    placed = (rows,) * 5 + (P("batch"),) * 3
    return jax.shard_map(body, mesh=mesh, in_specs=placed, out_specs=rows, check_vma=False)
```

```python
import math

import jax
import jax.numpy as jnp
from jax import lax
from jax.experimental import pallas as pl
from jax.experimental.pallas import tpu as pltpu
from jax.sharding import PartitionSpec as P

NEG=-1e30
C=512
U=4
LIM=40
V=3
QT=0
SCALE=(128**-0.5)*math.log2(math.e)
def attn_body(start_ref, plen_ref, win_ref, recv, out_ref, k_s, v_s, q_s, S0, S1, mx0, mx1, acc, tot, sems):
    S=(S0,S1); mx=(mx0,mx1)
    start=start_ref[0]; live=plen_ref[0]-start; win=win_ref[0]
    kmin=jnp.maximum(4096-start,0)
    groups=jnp.minimum((live+127)//128,8)
    def low(s): return jnp.maximum(4096+s*128-win+1,kmin)
    def clo(s): return low(s)//C
    def chi(s): return (4096+s*128+127)//C
    for s in range(8):
        k_s[s*512:(s+1)*512]=recv[s,512:1024]
        k_s[4096+s*128:4224+s*128]=recv[s,1536:1664]
        v_s[s]=recv[s,1024:1536].T
        v_s[8+s//4,:,(s%4)*128:(s%4+1)*128]=recv[s,1664:1792].T
        if QT: q_s[s]=recv[s,0:512].T
    def p1(s,b,c,masked):
        k=k_s[pl.ds(pl.multiple_of(c*C,C),C),:]
        if QT: sc=jnp.dot(k,q_s[s],preferred_element_type=jnp.float32)
        else: sc=lax.dot_general(k,recv[s,0:512],(((1,),(1,)),((),())),preferred_element_type=jnp.float32)
        if masked:
            row=lax.broadcasted_iota(jnp.int32,(C,128),0); lane=lax.broadcasted_iota(jnp.int32,(C,128),1)
            t=lane-row+(4096+s*128-c*C)
            ok=(t>=0)&(t<win)&(row>=kmin-c*C)
            sc=jnp.concatenate([jnp.where(ok,sc[:,h*128:(h+1)*128],NEG) for h in range(4)],1)
        S[b][c]=sc
        mx[b][...]=jnp.maximum(mx[b][...],jnp.max(sc.reshape(C//8,8,512),axis=0))
    def p2(b,c):
        p=jnp.exp2((S[b][c].reshape(C//8,8,512)-mx[b][...][None])*SCALE)
        tot[...]+=jnp.sum(p,axis=0)
        acc[...]+=jnp.dot(v_s[c],p.reshape(C,512).astype(jnp.bfloat16),preferred_element_type=jnp.float32)
    def init(b): mx[b][...]=jnp.full((8,512),NEG,jnp.float32)
    def zero():
        acc[...]=jnp.zeros_like(acc); tot[...]=jnp.zeros_like(tot)
    def top(b): mx[b][...]=jnp.broadcast_to(jnp.max(mx[b][...],axis=0,keepdims=True),(8,512))
    def fin(s):
        o=acc[...]/jnp.sum(tot[...],axis=0,keepdims=True)
        o=o.T
        i=lax.broadcasted_iota(jnp.int32,(4,128,128),1).reshape(512,128)
        out_ref[s]=jnp.where(i+s*128<live,o,0.0).astype(jnp.bfloat16)
    def loop(a,b,f): lax.fori_loop(a,b,lambda c,_:(f(c),0)[1],0)
    def unrolled(a,e,f,n=U):
        k=(e-a)//n
        loop(0,k,lambda j:f(a+n*j,n))
        if n>1: loop(a+n*k,e,lambda c:f(c,1))
    def first(c,n):
        for u in range(n): p1(0,0,c+u,True)
    def final(b):
        def f(c,n):
            for u in range(n): p2(b,c+u)
        return f
    def stage(s1,s2,b1,b2):
        init(b1); zero()
        a,e1,e2=clo(s1),chi(s1),chi(s2)
        loop(clo(s2),a,lambda c:p2(b2,c))
        lo=jnp.maximum((low(s1)+127+C-1)//C,a)
        hi=jnp.minimum(e1,e2+1)
        def edge(j,n):
            for u in range(n):
                c=jnp.where(j+u<lo,j+u,j+u-lo+hi)
                p1(s1,b1,c,True); p2(b2,c)
        unrolled(a,lo+e2+1-hi,edge,2)
        def both(c,n):
            for u in range(n):
                p1(s1,b1,c+u,False); p2(b2,c+u)
        n=(hi-lo)//U
        loop(0,n,lambda j:both(lo+U*j,U))
        at=lo+n*U
        for size in (3,2,1):
            more=(hi-at)//size
            loop(0,more,lambda j,at=at,size=size:both(at+size*j,size))
            at=at+size*more
        loop(e2+1,e1+1,lambda c:p1(s1,b1,c,True))
        top(b1); fin(s2)
    init(0)
    unrolled(clo(0),chi(0)+1,first,V)
    top(0)
    def pair(u,_):
        t=2*u+1
        @pl.when(t<groups)
        def _(): stage(t,t-1,1,0)
        @pl.when(t+1<groups)
        def _(): stage(t+1,t,0,1)
        return 0
    lax.fori_loop(0,groups//2,pair,0)
    last=groups-1
    zero()
    @pl.when(lax.rem(last,2)==0)
    def _(): unrolled(clo(last),chi(last)+1,final(0),V)
    @pl.when(lax.rem(last,2)==1)
    def _(): unrolled(clo(last),chi(last)+1,final(1),V)
    fin(last)
    def dead(s): out_ref[s]=jnp.zeros((512,128),jnp.bfloat16)
    loop(groups,8,dead)

def attn(start,plen,win,recv):
    return pl.pallas_call(attn_body,
        out_shape=jax.ShapeDtypeStruct((8,512,128),jnp.bfloat16),
        in_specs=[pl.BlockSpec(memory_space=pltpu.SMEM)]*3+[pl.BlockSpec(memory_space=pltpu.VMEM)],
        out_specs=pl.BlockSpec(memory_space=pltpu.VMEM),
        scratch_shapes=[pltpu.VMEM((5120,128),jnp.bfloat16),pltpu.VMEM((10,128,512),jnp.bfloat16),pltpu.VMEM((8,128,512),jnp.bfloat16),
            pltpu.VMEM((10,512,C),jnp.float32),pltpu.VMEM((10,512,C),jnp.float32),pltpu.VMEM((8,512),jnp.float32),pltpu.VMEM((8,512),jnp.float32),
            pltpu.VMEM((128,512),jnp.float32),pltpu.VMEM((8,512),jnp.float32),pltpu.SemaphoreType.DMA((40,))],
        compiler_params=pltpu.CompilerParams(vmem_limit_bytes=LIM<<20),
        cost_estimate=pl.CostEstimate(flops=2*2*4096*4352*128,bytes_accessed=5<<20,transcendentals=4096*4352),
        name="attend")(start,plen,win,recv)


def pack_body(q, sk, sv, ck, cv, out, qv, skv, svv, ckv, cvv, in_sems, sems):
    loads = [
        pltpu.make_async_copy(a, b, in_sems.at[i])
        for i, (a, b) in enumerate([(q, qv), (ck, ckv), (cv, cvv), (sk, skv), (sv, svv)])
    ]
    for c in loads:
        c.start()
    stores = []

    def cp(src, dst):
        c = pltpu.make_async_copy(src, dst, sems.at[len(stores)])
        c.start()
        stores.append(c)

    loads[0].wait()
    for e in range(8):
        for h in range(4):
            cp(qv.at[:, pl.ds((e * 4 + h) * 128, 128)], out.at[e, pl.ds(h * 128, 128)])
    for i, (v, at, count) in enumerate([(ckv, 512, 512), (cvv, 1024, 512), (skv, 1536, 128), (svv, 1664, 128)]):
        loads[1 + i].wait()
        for e in range(8):
            cp(v.at[:, pl.ds(e * 128, 128)], out.at[e, pl.ds(at, count)])
    for c in stores:
        c.wait()


def pack(*arrays):
    return pl.pallas_call(
        pack_body,
        out_shape=jax.ShapeDtypeStruct((8, 1792, 128), jnp.bfloat16),
        in_specs=[pl.BlockSpec(memory_space=pl.ANY)] * 5,
        out_specs=pl.BlockSpec(memory_space=pl.ANY),
        scratch_shapes=[pltpu.VMEM(a.shape, a.dtype) for a in arrays]
        + [pltpu.SemaphoreType.DMA((5,)), pltpu.SemaphoreType.DMA((64,))],
        compiler_params=pltpu.CompilerParams(vmem_limit_bytes=60 << 20),
        name="pack",
    )(*arrays)


def unpack_body(x, out):
    for s in range(x.shape[0]):
        for h in range(4):
            at = (s * 4 + h) * 128
            out[:, at : at + 128] = x[s, h * 128 : (h + 1) * 128]


def unpack(x):
    return pl.pallas_call(
        unpack_body,
        grid=(2,),
        out_shape=jax.ShapeDtypeStruct((128, 4096), jnp.bfloat16),
        in_specs=[pl.BlockSpec((4, 512, 128), lambda i: (i, 0, 0))],
        out_specs=pl.BlockSpec((128, 2048), lambda i: (0, i)),
        compiler_params=pltpu.CompilerParams(vmem_limit_bytes=16 << 20),
        name="unpack",
    )(x)


def body(queries, span_keys, span_values, cache_keys, cache_values, span_start, prompt_length, window_size):
    sent = pack(queries, span_keys, span_values, cache_keys, cache_values)
    got = lax.all_to_all(sent, "seq", split_axis=0, concat_axis=0, tiled=True)
    mixed = attn(span_start, prompt_length, window_size, got)
    back = lax.all_to_all(mixed, "seq", split_axis=0, concat_axis=0, tiled=True)
    return unpack(back)


def solution(mesh):
    rows = P(("batch", "seq"), None)
    placed = (rows,) * 5 + (P("batch"),) * 3
    return jax.shard_map(body, mesh=mesh, in_specs=placed, out_specs=rows, check_vma=False)
```
